32 devices in a mesh: row: 4 (over z), col: 8 (over y, x, core).
Axes of the slice: x: 2, y: 2, z: 4, core: 2. Of those that a mesh axis runs over, the one named last changes fastest.
Arguments:
- amplitudes: bfloat16 [512, 8, 4096], P('col', None, 'row'), may hold values from -6 to 6
- integrals: bfloat16 [32, 4096, 4096], P(None, 'row', 'col'), may hold values from -0.046875 to 0.046875
- blocks: int32 [32, 2], replicated, may hold values from 0 to 7, as said below
Outputs:
- ladder: bfloat16 [512, 8, 4096], P(('row', 'col'))
The draws below stay inside these ranges and needn't reach their ends.
Inputs may be any that keep to these rules, and one draw needn't show every extreme that they name: No (contracted tile, output tile) pair appears twice; each of the 8 contracted tiles and each output tile appears in exactly 4 blocks.
All inputs are finite; a program needn't handle non-finite values.
Results may differ from the reference program's by a relative error of at most 0.001.
Values may be sent and summed in bfloat16 or wider, within the bound.
A program may use at most 192 MiB of HBM per device.

```python
import jax
import jax.numpy as jnp
from jax import lax

PAIR_WIDTH = 4096
PAIR_TILES = 8
BLOCKS = 32
BLK_PER_Q = 4
PAIRS = 512


def draw_blocks(key, part):
    key_rows, key_cols, key_shuffle = jax.random.split(jax.random.fold_in(key, 17), 3)
    row_perm = jax.random.permutation(key_rows, PAIR_TILES)
    col_perm = jax.random.permutation(key_cols, PAIR_TILES)
    lanes = jnp.arange(BLOCKS) % PAIR_TILES
    turns = jnp.arange(BLOCKS) // PAIR_TILES
    table = jnp.stack([row_perm[lanes], col_perm[(lanes + turns) % PAIR_TILES]], axis=1)
    shuffle = jax.random.permutation(key_shuffle, BLOCKS)
    return table[shuffle].astype(jnp.int32)


def block_levels(stream_key, dims, cuts, least, top_value):
    def one(position, shards_of):
        draws = jax.random.uniform(jax.random.fold_in(jax.random.fold_in(stream_key, 6), position), (shards_of,), jnp.float32, least / len(cuts), top_value / len(cuts))
        return jnp.repeat(jnp.exp(draws), dims[position] // shards_of).reshape((-1,) + (1,) * (len(dims) - position - 1))

    level = one(*cuts[0])
    for cut in cuts[1:]:
        level = level * one(*cut)
    return level


def normal_values(key, extent, deviation, bound, shards=(), held_as=jnp.bfloat16):
    gain = block_levels(key, extent, shards, -0.22, 0.18) if shards else 1.0
    array = jax.random.normal(key, extent, jnp.float32) * deviation * gain
    return jnp.minimum(jnp.maximum(array, -bound), bound).astype(held_as)


def setup_inputs(seed: int = 0) -> dict:
    arg_keys = jax.random.split(jax.random.key(seed), 4)
    return {
        "amplitudes": normal_values(arg_keys[0], (PAIRS, PAIR_TILES, PAIR_WIDTH), 1.0, 6.0, ((0, 8), (2, 4))),
        "integrals": normal_values(arg_keys[1], (BLOCKS, PAIR_WIDTH, PAIR_WIDTH), (BLK_PER_Q * PAIR_WIDTH) ** -0.5, 0.046875, ((1, 4), (2, 8))),
        "blocks": draw_blocks(jax.random.fold_in(arg_keys[3], 71), 0),
    }


def reference(amplitudes, integrals, blocks):
    running = jnp.zeros((PAIRS, PAIR_TILES, PAIR_WIDTH), jnp.float32)

    def add_block(which_block, running):
        row_tile = blocks[which_block, 0].astype(jnp.int32)
        col_tile = blocks[which_block, 1].astype(jnp.int32)
        left_rows = lax.dynamic_index_in_dim(amplitudes, row_tile, 1, keepdims=False).astype(jnp.float32)
        right_cols = lax.dynamic_index_in_dim(integrals, which_block, 0, keepdims=False).astype(jnp.float32)
        product = jnp.dot(left_rows, right_cols, preferred_element_type=jnp.float32)
        current = lax.dynamic_index_in_dim(running, col_tile, 1, keepdims=False)
        return lax.dynamic_update_index_in_dim(running, current + product, col_tile, 1)

    running = lax.fori_loop(jnp.int32(0), jnp.int32(BLOCKS), add_block, running)
    return running.astype(jnp.bfloat16)
```

```python
import functools

import jax
import jax.numpy as jnp
from jax import lax
from jax.experimental import pallas as pl
from jax.experimental.pallas import tpu as pltpu
from jax.sharding import PartitionSpec as P

MESH = pl.DeviceIdType.MESH
STEPS = 32767.0
LANES = 128
SUBS = 4
SLICES = ((0, 1), (1, 1), (2, 2))
ORDERS = (
    ((2, 3, 1, 0), (3, 2, 1, 0)),
    ((2, 0, 3, 1), (3, 2, 0, 1)),
    ((0, 1, 3, 2), (1, 3, 0, 2)),
    ((0, 1, 2, 3), (1, 0, 2, 3)),
)


def flip(index, bit):
    return index + bit - 2 * bit * ((index // bit) % 2)


def group_order(R, r, q):
    if R != 4:
        return [g + 0 * r for g in range(R)]
    odd = q % 2
    low, high = r % 2, r // 2
    planes = ((1 - low) * (1 - high), low * (1 - high), (1 - low) * high, low * high)
    order = []
    for place in range(4):
        group = 0
        for plane in range(4):
            even_one, odd_one = ORDERS[plane][0][place], ORDERS[plane][1][place]
            group = group + planes[plane] * (even_one + odd * (odd_one - even_one))
        order.append(group)
    return order


def kernel(
    sizes,
    order_ref,
    amp_ref,
    int_ref,
    out_ref,
    held,
    work,
    blocks_vmem,
    acc,
    fin,
    send_q,
    recv_q,
    last_q,
    send_s,
    recv_s,
    last_s,
    int_sem,
    gather_send,
    gather_recv,
    sib_recv,
    zq_send,
    zs_send,
    zq_recv,
    zs_recv,
    lq_recv,
    ls_recv,
    out_send,
    out_recv,
):
    R, C, tiles, per, sub = sizes
    chips = C // 2
    rows = held.shape[2]
    width = acc.shape[1]
    share = out_ref.shape[1]

    r = lax.axis_index("row")
    c = lax.axis_index("col")
    q = c // 2
    core = c % 2
    sibling = 2 * q + 1 - core

    blocks_copy = pltpu.make_async_copy(int_ref, blocks_vmem, int_sem)
    blocks_copy.start()

    barrier = pltpu.get_barrier_semaphore()
    for step in range(1, C):
        pl.semaphore_signal(
            barrier, inc=1, device_id=(r, (c + step) % C), device_id_type=MESH
        )

    @pl.when(r > 0)
    def _():
        pl.semaphore_signal(barrier, inc=1, device_id=(r - 1, c), device_id_type=MESH)

    @pl.when(r < R - 1)
    def _():
        pl.semaphore_signal(barrier, inc=1, device_id=(r + 1, c), device_id_type=MESH)

    ends = (R - 1 - r) // (R - 1) + r // (R - 1)
    pl.semaphore_wait(barrier, C + 1 - ends)

    def place(group, s, of_core):
        first = pl.multiple_of((2 * s + of_core) * sub, sub)
        return held.at[:, group, pl.ds(first, sub)]

    def own_rows(s):
        return amp_ref.at[:, pl.ds(s * sub, sub)]

    def own_copy(s):
        return pltpu.make_async_copy(own_rows(s), place(q, s, core), gather_recv.at[q, s])

    def to_chip(k, s):
        there = q
        bit = 1
        while bit < chips:
            if k & bit:
                there = flip(there, bit)
            bit *= 2
        return pltpu.make_async_remote_copy(
            src_ref=own_rows(s),
            dst_ref=place(q, s, core),
            send_sem=gather_send,
            recv_sem=gather_recv.at[q, s],
            device_id=(r, 2 * there + core),
            device_id_type=MESH,
        )

    def to_sibling(group, s, own):
        return pltpu.make_async_remote_copy(
            src_ref=own_rows(s) if own else place(group, s, core),
            dst_ref=place(group, s, core),
            send_sem=gather_send,
            recv_sem=sib_recv.at[group, s],
            device_id=(r, sibling),
            device_id_type=MESH,
        )

    near = [1 << i for i in range(chips.bit_length() - 1)]
    far = [k for k in range(1, chips) if k not in near]

    def fetch(group, subs):
        for s in subs:
            here = place(group, s, core)
            pltpu.make_async_copy(here, here, gather_recv.at[group, s]).wait()

            @pl.when(group != q)
            def _():
                to_sibling(group, s, False).start()

    def fetched(group, subs):
        for s in subs:
            there = place(group, s, 1 - core)
            pltpu.make_async_copy(there, there, sib_recv.at[group, s]).wait()

    for s in range(SUBS):
        to_sibling(q, s, True).start()
        own_copy(s).start()
    for s in range(SUBS):
        for k in reversed(near):
            to_chip(k, s).start()

    def columns(who):
        return pl.ds(pl.multiple_of(who * width, width), width)

    def span(n):
        first, count = SLICES[n]
        return 2 * sub * first, 2 * sub * count

    def decoded(code, scale):
        scale = jnp.concatenate([scale] * (width // LANES), axis=1)
        return code.astype(jnp.int32).astype(jnp.float32) * scale

    def add_arrived(group, tile, slices, base):
        main = jnp.logical_or(
            jnp.logical_and(group >= r, r > 0),
            jnp.logical_and(group < r, r < R - 1),
        )

        @pl.when(main)
        def _():
            for n in slices:
                low, m = span(n)
                block = recv_q.at[group, tile, pl.ds(low, m)]
                scale = recv_s.at[group, n, tile]
                pltpu.make_async_copy(block, block, zq_recv.at[group, n, tile]).wait()
                pltpu.make_async_copy(scale, scale, zs_recv.at[group, n, tile]).wait()
                acc[pl.ds(low - base, m)] += decoded(block[...], scale[...])

        @pl.when(jnp.logical_and(group == r, r < R - 1))
        def _():
            for n in slices:
                low, m = span(n)
                block = last_q.at[tile, pl.ds(low, m)]
                scale = last_s.at[n, tile]
                pltpu.make_async_copy(block, block, lq_recv.at[n, tile]).wait()
                pltpu.make_async_copy(scale, scale, ls_recv.at[n, tile]).wait()
                acc[pl.ds(low - base, m)] += decoded(block[...], scale[...])

    def pass_on(group, tile, slices, base):
        for n in slices:
            low, m = span(n)
            x = acc[pl.ds(low - base, m)]
            peak = jnp.max(jnp.abs(x), axis=0, keepdims=True)
            most = peak[:, 0:LANES]
            for j in range(1, width // LANES):
                most = jnp.maximum(most, peak[:, j * LANES : (j + 1) * LANES])
            most = jnp.maximum(most, 1e-30)
            send_s[group, n, tile] = most * (1.0 / STEPS)
            steps = jnp.concatenate([STEPS / most] * (width // LANES), axis=1)
            code = jnp.round(x * steps).astype(jnp.int32).astype(jnp.int16)
            send_q[group, tile, pl.ds(low, m)] = code

            def copies(target, block, scale, block_sem, scale_sem):
                pltpu.make_async_remote_copy(
                    src_ref=send_q.at[group, tile, pl.ds(low, m)],
                    dst_ref=block,
                    send_sem=zq_send,
                    recv_sem=block_sem,
                    device_id=(target, c),
                    device_id_type=MESH,
                ).start()
                pltpu.make_async_remote_copy(
                    src_ref=send_s.at[group, n, tile],
                    dst_ref=scale,
                    send_sem=zs_send,
                    recv_sem=scale_sem,
                    device_id=(target, c),
                    device_id_type=MESH,
                ).start()

            main = (
                recv_q.at[group, tile, pl.ds(low, m)],
                recv_s.at[group, n, tile],
                zq_recv.at[group, n, tile],
                zs_recv.at[group, n, tile],
            )

            @pl.when(group > r)
            def _():
                copies(r + 1, *main)

            @pl.when(group < r - 1)
            def _():
                copies(r - 1, *main)

            @pl.when(group == r - 1)
            def _():
                copies(
                    r - 1,
                    last_q.at[tile, pl.ds(low, m)],
                    last_s.at[n, tile],
                    lq_recv.at[n, tile],
                    ls_recv.at[n, tile],
                )

    def deliver(tile, slices, base):
        for n in slices:
            low, m = span(n)
            fin[tile, pl.ds(low, m)] = acc[pl.ds(low - base, m)].astype(jnp.bfloat16)
            for at in range(low, low + m, share):
                s, of_core, inside = at // (2 * sub), (at // sub) % 2, at % sub
                target = (of_core * SUBS * sub + s * sub + inside) // share

                @pl.when(target != c)
                def _():
                    pltpu.make_async_remote_copy(
                        src_ref=fin.at[tile, pl.ds(at, share)],
                        dst_ref=out_ref.at[tile, :, columns(c)],
                        send_sem=out_send,
                        recv_sem=out_recv,
                        device_id=(r, target),
                        device_id_type=MESH,
                    ).start()

                @pl.when(target == c)
                def _():
                    pltpu.make_async_copy(
                        fin.at[tile, pl.ds(at, share)],
                        out_ref.at[tile, :, columns(c)],
                        out_recv,
                    ).start()

    def unit(group, slices, ahead):
        base = span(slices[0])[0]
        count = sum(span(n)[1] for n in slices)

        @pl.loop(0, tiles)
        def _(tile):
            work[tile, pl.ds(0, count)] = held[tile, group, pl.ds(base, count)]

        @pl.loop(0, tiles)
        def _(tile):
            if ahead is not None:

                @pl.when(tile == tiles - 1)
                def _():
                    ahead()

            total = None
            for j in range(per):
                block = order_ref[0, tile * per + j]
                pair_tile = order_ref[1, tile * per + j]
                part = jnp.dot(
                    work[pair_tile, pl.ds(0, count)],
                    blocks_vmem[block],
                    preferred_element_type=jnp.float32,
                )
                total = part if total is None else total + part
            acc[pl.ds(0, count)] = total
            add_arrived(group, tile, slices, base)

            @pl.when(group != r)
            def _():
                pass_on(group, tile, slices, base)

            @pl.when(group == r)
            def _():
                deliver(tile, slices, base)

    order = group_order(R, r, q)
    units = []
    for number, group in enumerate(order):
        if number < 2:
            units += [(group, (n,)) for n in range(len(SLICES))]
        else:
            units.append((group, tuple(range(len(SLICES)))))

    def subs_of(slices):
        first = SLICES[slices[0]][0]
        last = SLICES[slices[-1]]
        return range(first, last[0] + last[1])

    fetch(units[0][0], subs_of(units[0][1]))
    for number, (group, slices) in enumerate(units):
        if number == 2:
            for s in range(SUBS):
                for k in far:
                    to_chip(k, s).start()
        fetched(group, subs_of(slices))
        if number == 0:
            blocks_copy.wait()
        ahead = None
        if number + 1 < len(units):
            ahead = functools.partial(
                fetch, units[number + 1][0], subs_of(units[number + 1][1])
            )
        unit(group, slices, ahead)

    sent = held.at[:, :, pl.ds(0, rows - rows // C)]
    pltpu.make_async_copy(sent, sent, gather_send).wait()
    sent = send_q.at[pl.ds(0, R - 1)]
    pltpu.make_async_copy(sent, sent, zq_send).wait()
    sent = send_s.at[pl.ds(0, R - 1)]
    pltpu.make_async_copy(sent, sent, zs_send).wait()
    sent = out_ref.at[:, :, pl.ds(0, (C - 1) * width)]
    pltpu.make_async_copy(sent, sent, out_send).wait()
    pltpu.make_async_copy(out_ref, out_ref, out_recv).wait()


def on_device(R, C, amplitudes, integrals, blocks):
    pairs, tiles, inner = amplitudes.shape
    count, _, width = integrals.shape
    per = count // tiles
    share = pairs // R
    sub = pairs // SUBS
    rows = 2 * pairs
    pieces = len(SLICES)
    assert C == 2 * R and sub % share == 0 and share % 16 == 0

    key = blocks[:, 1] * count + jnp.arange(count, dtype=jnp.int32)
    rank = jnp.sum((key[:, None] > key[None, :]).astype(jnp.int32), axis=1)
    at = rank[:, None] == jnp.arange(count, dtype=jnp.int32)[None, :]
    both = jnp.stack([jnp.arange(count, dtype=jnp.int32), blocks[:, 0]], axis=0)
    order = jnp.sum(jnp.where(at[None], both[:, :, None], 0), axis=1)

    dma = pltpu.SemaphoreType.DMA
    out = pl.pallas_call(
        functools.partial(kernel, (R, C, tiles, per, sub)),
        out_shape=jax.ShapeDtypeStruct((tiles, share, C * width), jnp.bfloat16),
        in_specs=[
            pl.BlockSpec(memory_space=pltpu.SMEM),
            pl.BlockSpec(memory_space=pl.ANY),
            pl.BlockSpec(memory_space=pl.ANY),
        ],
        out_specs=pl.BlockSpec(memory_space=pltpu.VMEM),
        scratch_shapes=[
            pltpu.VMEM((tiles, R, rows, inner), jnp.bfloat16),
            pltpu.VMEM((tiles, rows, inner), jnp.bfloat16),
            pltpu.VMEM(integrals.shape, jnp.bfloat16),
            pltpu.VMEM((rows, width), jnp.float32),
            pltpu.VMEM((tiles, rows, width), jnp.bfloat16),
            pltpu.VMEM((R, tiles, rows, width), jnp.int16),
            pltpu.VMEM((R, tiles, rows, width), jnp.int16),
            pltpu.VMEM((tiles, rows, width), jnp.int16),
            pltpu.VMEM((R, pieces, tiles, 1, LANES), jnp.float32),
            pltpu.VMEM((R, pieces, tiles, 1, LANES), jnp.float32),
            pltpu.VMEM((pieces, tiles, 1, LANES), jnp.float32),
            dma,
            dma,
            dma((R, SUBS)),
            dma((R, SUBS)),
            dma,
            dma,
            dma((R, pieces, tiles)),
            dma((R, pieces, tiles)),
            dma((pieces, tiles)),
            dma((pieces, tiles)),
            dma,
            dma,
        ],
        compiler_params=pltpu.CompilerParams(
            collective_id=0, has_side_effects=True, vmem_limit_bytes=67043328
        ),
    )(order, amplitudes.transpose(1, 0, 2), integrals)
    return out.transpose(1, 0, 2)


def solution(mesh):
    return jax.shard_map(
        functools.partial(on_device, mesh.shape["row"], mesh.shape["col"]),
        mesh=mesh,
        in_specs=(P("col", None, "row"), P(None, "row", "col"), P()),
        out_specs=P(("row", "col"), None, None),
        check_vma=False,
    )
```

```python
import functools

import jax
import jax.numpy as jnp
from jax import lax
from jax.experimental import pallas as pl
from jax.experimental.pallas import tpu as pltpu
from jax.sharding import PartitionSpec as P

MESH = pl.DeviceIdType.MESH
STEPS = 32767.0
LANES = 128
SUBS = 4
END_UNITS = (2, 2, 2, 2, 2, 2, 4)
END_ORDER = (
    (8, 4, 9, 5, 10, 11, 12, 13, 14, 15, 6, 7, 0, 1, 2, 3),
    (4, 5, 12, 13, 14, 15, 8, 9, 10, 11, 6, 7, 0, 1, 2, 3),
    (8, 9, 12, 13, 14, 15, 10, 11, 4, 5, 6, 7, 0, 1, 2, 3),
    (12, 13, 14, 15, 8, 9, 10, 11, 4, 5, 6, 7, 0, 1, 2, 3),
)
INNER_UNITS = (4, 4, 4, 2, 2)
INNER_ORDER = (
    (8, 9, 0, 1, 10, 11, 2, 3, 12, 13, 4, 5, 14, 15, 6, 7),
    (12, 13, 4, 5, 14, 15, 0, 1, 8, 9, 2, 3, 10, 11, 6, 7),
    (8, 9, 12, 13, 14, 15, 0, 1, 10, 11, 2, 3, 4, 5, 6, 7),
    (12, 13, 14, 15, 8, 9, 10, 11, 0, 1, 4, 5, 2, 3, 6, 7),
)


def flip(index, bit):
    return index + bit - 2 * bit * ((index // bit) % 2)


def slices_in_order(table, r, q):
    upper = r // 2
    chip = q + upper * (3 - 2 * q)
    low, high = chip % 2, chip // 2
    slices = []
    for a, b, c, d in zip(*table):
        code = a + low * (b - a) + high * (c - a) + low * high * (a + d - b - c)
        group, s = code // SUBS, code % SUBS
        slices.append((group + upper * (3 - 2 * group), s))
    return slices


def kernel(
    sizes,
    order,
    amp_ref,
    int_ref,
    out_ref,
    held,
    work,
    blocks_vmem,
    acc,
    fin,
    send_q,
    recv_q,
    send_s,
    recv_s,
    int_sem,
    gather_send,
    gather_recv,
    sib_recv,
    zq_send,
    zs_send,
    zq_recv,
    zs_recv,
    out_send,
    out_recv,
):
    R, C, tiles, per, sub = sizes
    chips = C // 2
    rows = held.shape[2]
    slab = 2 * sub
    width = acc.shape[1]
    share = out_ref.shape[1]

    r = lax.axis_index("row")
    c = lax.axis_index("col")
    q = c // 2
    core = c % 2
    sibling = 2 * q + 1 - core

    def place(group, s, of_core):
        first = pl.multiple_of((2 * s + of_core) * sub, sub)
        return held.at[:, group, pl.ds(first, sub)]

    def own_copy(s):
        return pltpu.make_async_copy(
            amp_ref.at[:, pl.ds(s * sub, sub)], place(q, s, core), gather_recv.at[q, s]
        )

    for s in range(SUBS):
        own_copy(s).start()
    blocks_copy = pltpu.make_async_copy(int_ref, blocks_vmem, int_sem)
    blocks_copy.start()

    barrier = pltpu.get_barrier_semaphore()
    for step in range(1, C):
        pl.semaphore_signal(
            barrier, inc=1, device_id=(r, (c + step) % C), device_id_type=MESH
        )

    @pl.when(r > 0)
    def _():
        pl.semaphore_signal(barrier, inc=1, device_id=(r - 1, c), device_id_type=MESH)

    @pl.when(r < R - 1)
    def _():
        pl.semaphore_signal(barrier, inc=1, device_id=(r + 1, c), device_id_type=MESH)

    ends = (R - 1 - r) // (R - 1) + r // (R - 1)
    pl.semaphore_wait(barrier, C + 1 - ends)

    def to_chip(k, s):
        there = q
        bit = 1
        while bit < chips:
            if k & bit:
                there = flip(there, bit)
            bit *= 2
        return pltpu.make_async_remote_copy(
            src_ref=place(q, s, core),
            dst_ref=place(q, s, core),
            send_sem=gather_send,
            recv_sem=gather_recv.at[q, s],
            device_id=(r, 2 * there + core),
            device_id_type=MESH,
        )

    def to_sibling(group, s):
        return pltpu.make_async_remote_copy(
            src_ref=place(group, s, core),
            dst_ref=place(group, s, core),
            send_sem=gather_send,
            recv_sem=sib_recv.at[group, s],
            device_id=(r, sibling),
            device_id_type=MESH,
        )

    near = [1 << i for i in range(chips.bit_length() - 1)]
    far = [k for k in range(1, chips) if k not in near]

    def send_far():
        for s in range(SUBS):
            for k in far:
                to_chip(k, s).start()

    def fetch(slices):
        for group, s in slices:

            @pl.when(group != q)
            def _():
                here = place(group, s, core)
                pltpu.make_async_copy(here, here, gather_recv.at[group, s]).wait()
                to_sibling(group, s).start()

    def fetched(slices):
        for group, s in slices:
            there = place(group, s, 1 - core)
            pltpu.make_async_copy(there, there, sib_recv.at[group, s]).wait()

    for s in range(SUBS):
        own_copy(s).wait()
        for k in reversed(near):
            to_chip(k, s).start()
        to_sibling(q, s).start()

    def columns(who):
        return pl.ds(pl.multiple_of(who * width, width), width)

    def slab_of(s):
        return pl.ds(pl.multiple_of(s * slab, slab), slab)

    def add_arrived(slot, s, tile, at):
        block = recv_q.at[slot, tile, slab_of(s)]
        scale = recv_s.at[slot, s, tile]
        pltpu.make_async_copy(block, block, zq_recv.at[slot, s, tile]).wait()
        pltpu.make_async_copy(scale, scale, zs_recv.at[slot, s, tile]).wait()
        lanes = jnp.concatenate([scale[...]] * (width // LANES), axis=1)
        acc[pl.ds(at, slab)] += block[...].astype(jnp.int32).astype(jnp.float32) * lanes

    def pass_on(group, s, tile, at):
        x = acc[pl.ds(at, slab)]
        peak = jnp.max(jnp.abs(x), axis=0, keepdims=True)
        most = peak[:, 0:LANES]
        for j in range(1, width // LANES):
            most = jnp.maximum(most, peak[:, j * LANES : (j + 1) * LANES])
        most = jnp.maximum(most, 1e-30)
        send_s[group, s, tile] = most * (1.0 / STEPS)
        steps = jnp.concatenate([STEPS / most] * (width // LANES), axis=1)
        send_q[group, tile, slab_of(s)] = (
            jnp.round(x * steps).astype(jnp.int32).astype(jnp.int16)
        )

        def copies(target, slot):
            pltpu.make_async_remote_copy(
                src_ref=send_q.at[group, tile, slab_of(s)],
                dst_ref=recv_q.at[slot, tile, slab_of(s)],
                send_sem=zq_send,
                recv_sem=zq_recv.at[slot, s, tile],
                device_id=(target, c),
                device_id_type=MESH,
            ).start()
            pltpu.make_async_remote_copy(
                src_ref=send_s.at[group, s, tile],
                dst_ref=recv_s.at[slot, s, tile],
                send_sem=zs_send,
                recv_sem=zs_recv.at[slot, s, tile],
                device_id=(target, c),
                device_id_type=MESH,
            ).start()

        @pl.when(group > r)
        def _():
            copies(r + 1, group)

        @pl.when(group < r - 1)
        def _():
            copies(r - 1, group)

        @pl.when(group == r - 1)
        def _():
            copies(r - 1, R)

    def deliver(s, tile, at):
        fin[tile, slab_of(s)] = acc[pl.ds(at, slab)].astype(jnp.bfloat16)
        for inside in range(0, slab, share):
            first = pl.multiple_of(s * slab + inside, share)
            source = fin.at[tile, pl.ds(first, share)]
            target = (inside // sub * SUBS + s) * (sub // share) + inside % sub // share

            @pl.when(target != c)
            def _():
                pltpu.make_async_remote_copy(
                    src_ref=source,
                    dst_ref=out_ref.at[tile, :, columns(c)],
                    send_sem=out_send,
                    recv_sem=out_recv,
                    device_id=(r, target),
                    device_id_type=MESH,
                ).start()

            @pl.when(target == c)
            def _():
                pltpu.make_async_copy(
                    source, out_ref.at[tile, :, columns(c)], out_recv
                ).start()

    def unit(slices, following, far_at):
        @pl.loop(0, tiles)
        def _(tile):
            for i, (group, s) in enumerate(slices):
                work[tile, pl.ds(i * slab, slab)] = held[tile, group, slab_of(s)]

        @pl.loop(0, tiles)
        def _(tile):
            if following:

                @pl.when(tile == tiles - 1)
                def _():
                    fetch(following)

            if far_at is not None:

                @pl.when(tile == far_at)
                def _():
                    send_far()

            total = None
            for j in range(per):
                part = jnp.dot(
                    work[order[1, tile * per + j], pl.ds(0, slab * len(slices))],
                    blocks_vmem[order[0, tile * per + j]],
                    preferred_element_type=jnp.float32,
                )
                total = part if total is None else total + part
            acc[pl.ds(0, slab * len(slices))] = total
            for i, (group, s) in enumerate(slices):
                at = i * slab

                @pl.when(
                    jnp.logical_or(
                        jnp.logical_and(group >= r, r > 0),
                        jnp.logical_and(group < r, r < R - 1),
                    )
                )
                def _():
                    add_arrived(group, s, tile, at)

                @pl.when(jnp.logical_and(group == r, r < R - 1))
                def _():
                    add_arrived(R, s, tile, at)

                @pl.when(group != r)
                def _():
                    pass_on(group, s, tile, at)

                @pl.when(group == r)
                def _():
                    deliver(s, tile, at)

    def run(slices, counts, far_unit):
        units = []
        first = 0
        for n in counts:
            units.append(slices[first : first + n])
            first += n
        fetch(units[0])
        for number, one in enumerate(units):
            fetched(one)
            unit(
                one,
                units[number + 1] if number + 1 < len(units) else [],
                tiles // 2 if number == far_unit else None,
            )

    blocks_copy.wait()
    if R == 4:
        at_end = r * (R - 1 - r) == 0

        @pl.when(at_end)
        def _():
            run(slices_in_order(END_ORDER, r, q), END_UNITS, 1)

        @pl.when(jnp.logical_not(at_end))
        def _():
            run(slices_in_order(INNER_ORDER, r, q), INNER_UNITS, 0)

    else:
        send_far()
        run([(g + 0 * r, s) for g in range(R) for s in range(SUBS)], (SUBS,) * R, None)

    sent = held.at[:, :, pl.ds(0, rows - rows // C)]
    pltpu.make_async_copy(sent, sent, gather_send).wait()
    sent = send_q.at[pl.ds(0, R - 1)]
    pltpu.make_async_copy(sent, sent, zq_send).wait()
    sent = send_s.at[pl.ds(0, R - 1)]
    pltpu.make_async_copy(sent, sent, zs_send).wait()
    sent = out_ref.at[:, :, pl.ds(0, (C - 1) * width)]
    pltpu.make_async_copy(sent, sent, out_send).wait()
    pltpu.make_async_copy(out_ref, out_ref, out_recv).wait()


def on_device(R, C, amplitudes, integrals, blocks):
    pairs, tiles, inner = amplitudes.shape
    count, _, width = integrals.shape
    per = count // tiles
    share = pairs // R
    sub = pairs // SUBS
    rows = 2 * pairs
    assert C == 2 * R and sub % share == 0 and share % 16 == 0

    key = blocks[:, 1] * count + jnp.arange(count, dtype=jnp.int32)
    rank = jnp.sum((key[:, None] > key[None, :]).astype(jnp.int32), axis=1)
    at = rank[:, None] == jnp.arange(count, dtype=jnp.int32)[None, :]
    both = jnp.stack([jnp.arange(count, dtype=jnp.int32), blocks[:, 0]], axis=0)
    order = jnp.sum(jnp.where(at[None], both[:, :, None], 0), axis=1)

    dma = pltpu.SemaphoreType.DMA
    out = pl.pallas_call(
        functools.partial(kernel, (R, C, tiles, per, sub)),
        out_shape=jax.ShapeDtypeStruct((tiles, share, C * width), jnp.bfloat16),
        in_specs=[
            pl.BlockSpec(memory_space=pltpu.SMEM),
            pl.BlockSpec(memory_space=pl.ANY),
            pl.BlockSpec(memory_space=pl.ANY),
        ],
        out_specs=pl.BlockSpec(memory_space=pltpu.VMEM),
        scratch_shapes=[
            pltpu.VMEM((tiles, R, rows, inner), jnp.bfloat16),
            pltpu.VMEM((tiles, rows, inner), jnp.bfloat16),
            pltpu.VMEM(integrals.shape, jnp.bfloat16),
            pltpu.VMEM((rows, width), jnp.float32),
            pltpu.VMEM((tiles, rows, width), jnp.bfloat16),
            pltpu.VMEM((R, tiles, rows, width), jnp.int16),
            pltpu.VMEM((R + 1, tiles, rows, width), jnp.int16),
            pltpu.VMEM((R, SUBS, tiles, 1, LANES), jnp.float32),
            pltpu.VMEM((R + 1, SUBS, tiles, 1, LANES), jnp.float32),
            dma,
            dma,
            dma((R, SUBS)),
            dma((R, SUBS)),
            dma,
            dma,
            dma((R + 1, SUBS, tiles)),
            dma((R + 1, SUBS, tiles)),
            dma,
            dma,
        ],
        compiler_params=pltpu.CompilerParams(
            collective_id=0, has_side_effects=True, vmem_limit_bytes=67043328
        ),
    )(order, amplitudes.transpose(1, 0, 2), integrals)
    return out.transpose(1, 0, 2)


def solution(mesh):
    return jax.shard_map(
        functools.partial(on_device, mesh.shape["row"], mesh.shape["col"]),
        mesh=mesh,
        in_specs=(P("col", None, "row"), P(None, "row", "col"), P()),
        out_specs=P(("row", "col"), None, None),
        check_vma=False,
    )
```

```python
import functools

import jax
import jax.numpy as jnp
from jax import lax
from jax.experimental import pallas as pl
from jax.experimental.pallas import tpu as pltpu
from jax.sharding import PartitionSpec as P

MESH = pl.DeviceIdType.MESH
STEPS = 32767.0
LANES = 128
SUBS = 4
TURNS = (0, 2, 1, 3)
END_UNITS = (2, 2, 2, 2, 2, 2, 2, 2)
END_ORDER = (
    (8, 4, 9, 5, 10, 11, 12, 13, 14, 15, 0, 1, 6, 7, 2, 3),
    (4, 5, 12, 13, 14, 15, 8, 9, 10, 11, 0, 1, 6, 7, 2, 3),
    (8, 9, 12, 13, 14, 15, 10, 11, 4, 5, 0, 1, 6, 7, 2, 3),
    (12, 13, 14, 15, 8, 9, 10, 11, 4, 5, 0, 1, 6, 7, 2, 3),
)
INNER_UNITS = (4, 4, 4, 2, 2)
INNER_ORDER = (
    (8, 9, 0, 1, 10, 11, 2, 3, 12, 13, 4, 5, 14, 15, 6, 7),
    (12, 13, 4, 5, 14, 15, 0, 1, 8, 9, 2, 3, 10, 11, 6, 7),
    (8, 9, 12, 13, 14, 15, 0, 1, 10, 11, 2, 3, 4, 5, 6, 7),
    (12, 13, 14, 15, 8, 9, 10, 11, 0, 1, 4, 5, 2, 3, 6, 7),
)


def flip(index, bit):
    return index + bit - 2 * bit * ((index // bit) % 2)


def slices_in_order(table, r, q):
    upper = r // 2
    chip = q + upper * (3 - 2 * q)
    low, high = chip % 2, chip // 2
    slices = []
    for codes in zip(*table):
        a, b, c, d = (SUBS * (x // SUBS) + TURNS[x % SUBS] for x in codes)
        code = a + low * (b - a) + high * (c - a) + low * high * (a + d - b - c)
        group, s = code // SUBS, code % SUBS
        slices.append((group + upper * (3 - 2 * group), s))
    return slices


def kernel(
    sizes,
    order,
    amp_ref,
    int_ref,
    out_ref,
    held,
    work,
    blocks_vmem,
    acc,
    fin,
    send_q,
    recv_q,
    send_s,
    recv_s,
    int_sem,
    gather_send,
    gather_recv,
    sib_recv,
    zq_send,
    zs_send,
    zq_recv,
    zs_recv,
    out_send,
    out_recv,
):
    R, C, tiles, per, sub = sizes
    chips = C // 2
    rows = held.shape[2]
    slab = 2 * sub
    width = acc.shape[1]
    share = out_ref.shape[1]

    r = lax.axis_index("row")
    c = lax.axis_index("col")
    q = c // 2
    core = c % 2
    sibling = 2 * q + 1 - core

    def place(group, s, of_core):
        first = pl.multiple_of((2 * s + of_core) * sub, sub)
        return held.at[:, group, pl.ds(first, sub)]

    def own_copy(s):
        return pltpu.make_async_copy(
            amp_ref.at[:, pl.ds(s * sub, sub)], place(q, s, core), gather_recv.at[q, s]
        )

    for s in range(SUBS):
        own_copy(s).start()
    for s in range(SUBS):
        own_copy(s).wait()
    blocks_copy = pltpu.make_async_copy(int_ref, blocks_vmem, int_sem)
    blocks_copy.start()

    barrier = pltpu.get_barrier_semaphore()
    for step in range(1, C):
        pl.semaphore_signal(
            barrier, inc=1, device_id=(r, (c + step) % C), device_id_type=MESH
        )

    @pl.when(r > 0)
    def _():
        pl.semaphore_signal(barrier, inc=1, device_id=(r - 1, c), device_id_type=MESH)

    @pl.when(r < R - 1)
    def _():
        pl.semaphore_signal(barrier, inc=1, device_id=(r + 1, c), device_id_type=MESH)

    ends = (R - 1 - r) // (R - 1) + r // (R - 1)
    pl.semaphore_wait(barrier, C + 1 - ends)

    def to_chip(k, s):
        there = q
        bit = 1
        while bit < chips:
            if k & bit:
                there = flip(there, bit)
            bit *= 2
        return pltpu.make_async_remote_copy(
            src_ref=place(q, s, core),
            dst_ref=place(q, s, core),
            send_sem=gather_send,
            recv_sem=gather_recv.at[q, s],
            device_id=(r, 2 * there + core),
            device_id_type=MESH,
        )

    def to_sibling(group, s):
        return pltpu.make_async_remote_copy(
            src_ref=place(group, s, core),
            dst_ref=place(group, s, core),
            send_sem=gather_send,
            recv_sem=sib_recv.at[group, s],
            device_id=(r, sibling),
            device_id_type=MESH,
        )

    near = [1 << i for i in range(chips.bit_length() - 1)]
    far = [k for k in range(1, chips) if k not in near]

    def send_far():
        for s in range(SUBS):
            for k in far:
                to_chip(k, s).start()

    def fetch(slices):
        for group, s in slices:

            @pl.when(group != q)
            def _():
                here = place(group, s, core)
                pltpu.make_async_copy(here, here, gather_recv.at[group, s]).wait()
                to_sibling(group, s).start()

    beside, above = flip(q, 1), flip(q, 2)
    corner = flip(beside, 2)

    def relay(group, s, there):
        pltpu.make_async_remote_copy(
            src_ref=place(group, s, core),
            dst_ref=place(group, s, core),
            send_sem=gather_send,
            recv_sem=gather_recv.at[group, s],
            device_id=(r, 2 * there + core),
            device_id_type=MESH,
        ).start()

    def near_arrives(turn):
        s = TURNS[turn]
        for group in (beside, above):
            here = place(group, s, core)
            pltpu.make_async_copy(here, here, gather_recv.at[group, s]).wait()
            to_sibling(group, s).start()
        if turn % 2 == 0:
            relay(beside, s, above)
        else:
            relay(above, s, beside)

    def corner_arrives(turn):
        s = TURNS[turn]
        here = place(corner, s, core)
        pltpu.make_async_copy(here, here, gather_recv.at[corner, s]).wait()
        to_sibling(corner, s).start()

    def fetched(slices):
        for group, s in slices:
            there = place(group, s, 1 - core)
            pltpu.make_async_copy(there, there, sib_recv.at[group, s]).wait()

    for s in TURNS:
        for k in reversed(near):
            to_chip(k, s).start()
        to_sibling(q, s).start()

    def columns(who):
        return pl.ds(pl.multiple_of(who * width, width), width)

    def slab_of(s):
        return pl.ds(pl.multiple_of(s * slab, slab), slab)

    def add_arrived(slot, s, tile, at):
        block = recv_q.at[slot, tile, slab_of(s)]
        scale = recv_s.at[slot, s, tile]
        pltpu.make_async_copy(block, block, zq_recv.at[slot, s, tile]).wait()
        pltpu.make_async_copy(scale, scale, zs_recv.at[slot, s, tile]).wait()
        lanes = jnp.concatenate([scale[...]] * (width // LANES), axis=1)
        acc[pl.ds(at, slab)] += block[...].astype(jnp.int32).astype(jnp.float32) * lanes

    def pass_on(group, s, tile, at):
        x = acc[pl.ds(at, slab)]
        peak = jnp.max(jnp.abs(x), axis=0, keepdims=True)
        most = peak[:, 0:LANES]
        for j in range(1, width // LANES):
            most = jnp.maximum(most, peak[:, j * LANES : (j + 1) * LANES])
        most = jnp.maximum(most, 1e-30)
        send_s[group, s, tile] = most * (1.0 / STEPS)
        steps = jnp.concatenate([STEPS / most] * (width // LANES), axis=1)
        send_q[group, tile, slab_of(s)] = (
            jnp.round(x * steps).astype(jnp.int32).astype(jnp.int16)
        )

        def copies(target, slot):
            pltpu.make_async_remote_copy(
                src_ref=send_q.at[group, tile, slab_of(s)],
                dst_ref=recv_q.at[slot, tile, slab_of(s)],
                send_sem=zq_send,
                recv_sem=zq_recv.at[slot, s, tile],
                device_id=(target, c),
                device_id_type=MESH,
            ).start()
            pltpu.make_async_remote_copy(
                src_ref=send_s.at[group, s, tile],
                dst_ref=recv_s.at[slot, s, tile],
                send_sem=zs_send,
                recv_sem=zs_recv.at[slot, s, tile],
                device_id=(target, c),
                device_id_type=MESH,
            ).start()

        @pl.when(group > r)
        def _():
            copies(r + 1, group)

        @pl.when(group < r - 1)
        def _():
            copies(r - 1, group)

        @pl.when(group == r - 1)
        def _():
            copies(r - 1, R)

    def deliver(s, tile, at):
        fin[tile, slab_of(s)] = acc[pl.ds(at, slab)].astype(jnp.bfloat16)
        for inside in range(0, slab, share):
            first = pl.multiple_of(s * slab + inside, share)
            source = fin.at[tile, pl.ds(first, share)]
            target = (inside // sub * SUBS + s) * (sub // share) + inside % sub // share

            @pl.when(target != c)
            def _():
                pltpu.make_async_remote_copy(
                    src_ref=source,
                    dst_ref=out_ref.at[tile, :, columns(c)],
                    send_sem=out_send,
                    recv_sem=out_recv,
                    device_id=(r, target),
                    device_id_type=MESH,
                ).start()

            @pl.when(target == c)
            def _():
                pltpu.make_async_copy(
                    source, out_ref.at[tile, :, columns(c)], out_recv
                ).start()

    def unit(slices, hooks):
        @pl.loop(0, tiles)
        def _(tile):
            for i, (group, s) in enumerate(slices):
                work[tile, pl.ds(i * slab, slab)] = held[tile, group, slab_of(s)]

        @pl.loop(0, tiles)
        def _(tile):
            for at, steps in hooks:

                @pl.when(tile == at)
                def _():
                    for step in steps:
                        step()

            total = None
            for j in range(per):
                part = jnp.dot(
                    work[order[1, tile * per + j], pl.ds(0, slab * len(slices))],
                    blocks_vmem[order[0, tile * per + j]],
                    preferred_element_type=jnp.float32,
                )
                total = part if total is None else total + part
            acc[pl.ds(0, slab * len(slices))] = total
            for i, (group, s) in enumerate(slices):
                at = i * slab

                @pl.when(
                    jnp.logical_or(
                        jnp.logical_and(group >= r, r > 0),
                        jnp.logical_and(group < r, r < R - 1),
                    )
                )
                def _():
                    add_arrived(group, s, tile, at)

                @pl.when(jnp.logical_and(group == r, r < R - 1))
                def _():
                    add_arrived(R, s, tile, at)

                @pl.when(group != r)
                def _():
                    pass_on(group, s, tile, at)

                @pl.when(group == r)
                def _():
                    deliver(s, tile, at)

    def run(slices, counts, hooks):
        first = 0
        for number, n in enumerate(counts):
            one = slices[first : first + n]
            first += n
            for at, steps in hooks[number]:
                if at < 0:
                    for step in steps:
                        step()
            fetched(one)
            unit(one, [hook for hook in hooks[number] if hook[0] >= 0])

    def steps(function, *turns):
        return [functools.partial(function, turn) for turn in turns]

    if R == 4:
        at_end = r * (R - 1 - r) == 0
        last = tiles - 1

        @pl.when(at_end)
        def _():
            hooks = [[] for _ in END_UNITS]
            hooks[0] = [(-1, steps(near_arrives, 0)), (last, steps(near_arrives, 1))]
            hooks[1] = [(last // 2, steps(near_arrives, 2)), (last, steps(near_arrives, 3))]
            hooks[2] = [(last, steps(corner_arrives, 0, 1))]
            hooks[3] = [(last, steps(corner_arrives, 2, 3))]
            hooks[0][0][1].append(blocks_copy.wait)
            run(slices_in_order(END_ORDER, r, q), END_UNITS, hooks)

        @pl.when(jnp.logical_not(at_end))
        def _():
            hooks = [[] for _ in INNER_UNITS]
            hooks[0] = [
                (-1, steps(near_arrives, 0, 1)),
                (1, steps(near_arrives, 2)),
                (last, steps(near_arrives, 3)),
            ]
            hooks[1] = [
                (last // 2, steps(corner_arrives, 0, 1)),
                (last, steps(corner_arrives, 2, 3)),
            ]
            hooks[0][0][1].append(blocks_copy.wait)
            run(slices_in_order(INNER_ORDER, r, q), INNER_UNITS, hooks)

    else:
        send_far()
        groups = [[(g + 0 * r, s) for s in range(SUBS)] for g in range(R)]
        hooks = [[(-1, [functools.partial(fetch, group)])] for group in groups]
        hooks[0][0][1].append(blocks_copy.wait)
        run(sum(groups, []), (SUBS,) * R, hooks)

    sent = held.at[:, :, pl.ds(0, rows - rows // C)]
    pltpu.make_async_copy(sent, sent, gather_send).wait()
    sent = send_q.at[pl.ds(0, R - 1)]
    pltpu.make_async_copy(sent, sent, zq_send).wait()
    sent = send_s.at[pl.ds(0, R - 1)]
    pltpu.make_async_copy(sent, sent, zs_send).wait()
    sent = out_ref.at[:, :, pl.ds(0, (C - 1) * width)]
    pltpu.make_async_copy(sent, sent, out_send).wait()
    pltpu.make_async_copy(out_ref, out_ref, out_recv).wait()


def on_device(R, C, amplitudes, integrals, blocks):
    pairs, tiles, inner = amplitudes.shape
    count, _, width = integrals.shape
    per = count // tiles
    share = pairs // R
    sub = pairs // SUBS
    rows = 2 * pairs
    assert C == 2 * R and sub % share == 0 and share % 16 == 0

    key = blocks[:, 1] * count + jnp.arange(count, dtype=jnp.int32)
    rank = jnp.sum((key[:, None] > key[None, :]).astype(jnp.int32), axis=1)
    at = rank[:, None] == jnp.arange(count, dtype=jnp.int32)[None, :]
    both = jnp.stack([jnp.arange(count, dtype=jnp.int32), blocks[:, 0]], axis=0)
    order = jnp.sum(jnp.where(at[None], both[:, :, None], 0), axis=1)

    dma = pltpu.SemaphoreType.DMA
    out = pl.pallas_call(
        functools.partial(kernel, (R, C, tiles, per, sub)),
        out_shape=jax.ShapeDtypeStruct((tiles, share, C * width), jnp.bfloat16),
        in_specs=[
            pl.BlockSpec(memory_space=pltpu.SMEM),
            pl.BlockSpec(memory_space=pl.ANY),
            pl.BlockSpec(memory_space=pl.ANY),
        ],
        out_specs=pl.BlockSpec(memory_space=pltpu.VMEM),
        scratch_shapes=[
            pltpu.VMEM((tiles, R, rows, inner), jnp.bfloat16),
            pltpu.VMEM((tiles, rows, inner), jnp.bfloat16),
            pltpu.VMEM(integrals.shape, jnp.bfloat16),
            pltpu.VMEM((rows, width), jnp.float32),
            pltpu.VMEM((tiles, rows, width), jnp.bfloat16),
            pltpu.VMEM((R, tiles, rows, width), jnp.int16),
            pltpu.VMEM((R + 1, tiles, rows, width), jnp.int16),
            pltpu.VMEM((R, SUBS, tiles, 1, LANES), jnp.float32),
            pltpu.VMEM((R + 1, SUBS, tiles, 1, LANES), jnp.float32),
            dma,
            dma,
            dma((R, SUBS)),
            dma((R, SUBS)),
            dma,
            dma,
            dma((R + 1, SUBS, tiles)),
            dma((R + 1, SUBS, tiles)),
            dma,
            dma,
        ],
        compiler_params=pltpu.CompilerParams(
            collective_id=0, has_side_effects=True, vmem_limit_bytes=67043328
        ),
    )(order, amplitudes.transpose(1, 0, 2), integrals)
    return out.transpose(1, 0, 2)


def solution(mesh):
    return jax.shard_map(
        functools.partial(on_device, mesh.shape["row"], mesh.shape["col"]),
        mesh=mesh,
        in_specs=(P("col", None, "row"), P(None, "row", "col"), P()),
        out_specs=P(("row", "col"), None, None),
        check_vma=False,
    )
```

```python
import functools

import jax
import jax.numpy as jnp
from jax import lax
from jax.experimental import pallas as pl
from jax.experimental.pallas import tpu as pltpu
from jax.sharding import PartitionSpec as P

MESH = pl.DeviceIdType.MESH
STEPS = 32767.0
LANES = 128
SUBS = 4
TURNS = (0, 2, 1, 3)
END_UNITS = (2, 2, 2, 2, 2, 2, 2, 2)
END_ORDER = (
    (8, 4, 9, 5, 12, 13, 14, 15, 10, 11, 0, 1, 6, 7, 2, 3),
    (4, 5, 12, 13, 14, 15, 8, 9, 10, 11, 0, 1, 6, 7, 2, 3),
    (8, 9, 12, 13, 14, 15, 10, 11, 4, 5, 0, 1, 6, 7, 2, 3),
    (12, 13, 14, 15, 8, 9, 10, 11, 4, 5, 0, 1, 6, 7, 2, 3),
)
INNER_UNITS = (2, 2, 4, 4, 2, 2)
INNER_ORDER = (
    (8, 0, 9, 1, 12, 13, 2, 3, 14, 15, 4, 5, 10, 11, 6, 7),
    (12, 13, 4, 5, 14, 15, 0, 1, 8, 9, 2, 3, 10, 11, 6, 7),
    (8, 9, 12, 13, 14, 15, 0, 1, 10, 11, 2, 3, 4, 5, 6, 7),
    (12, 13, 14, 15, 8, 9, 0, 1, 10, 11, 2, 3, 4, 5, 6, 7),
)


def flip(index, bit):
    return index + bit - 2 * bit * ((index // bit) % 2)


def slices_in_order(table, r, q):
    upper = r // 2
    chip = q + upper * (3 - 2 * q)
    low, high = chip % 2, chip // 2
    slices = []
    for codes in zip(*table):
        a, b, c, d = (SUBS * (x // SUBS) + TURNS[x % SUBS] for x in codes)
        code = a + low * (b - a) + high * (c - a) + low * high * (a + d - b - c)
        group, s = code // SUBS, code % SUBS
        slices.append((group + upper * (3 - 2 * group), s))
    return slices


def kernel(
    sizes,
    order,
    amp_ref,
    int_ref,
    out_ref,
    held,
    work,
    blocks_vmem,
    acc,
    fin,
    send_q,
    recv_q,
    send_s,
    recv_s,
    int_sem,
    gather_send,
    gather_recv,
    sib_recv,
    zq_send,
    zs_send,
    zq_recv,
    zs_recv,
    out_send,
    out_recv,
):
    R, C, tiles, per, sub = sizes
    chips = C // 2
    rows = held.shape[2]
    slab = 2 * sub
    width = acc.shape[1]
    share = out_ref.shape[1]

    r = lax.axis_index("row")
    c = lax.axis_index("col")
    q = c // 2
    core = c % 2
    sibling = 2 * q + 1 - core

    def place(group, s, of_core):
        first = pl.multiple_of((2 * s + of_core) * sub, sub)
        return held.at[:, group, pl.ds(first, sub)]

    def own_copy(s):
        return pltpu.make_async_copy(
            amp_ref.at[:, pl.ds(s * sub, sub)], place(q, s, core), gather_recv.at[q, s]
        )

    for s in range(SUBS):
        own_copy(s).start()
    for s in range(SUBS):
        own_copy(s).wait()
    blocks_copy = pltpu.make_async_copy(int_ref, blocks_vmem, int_sem)
    blocks_copy.start()

    barrier = pltpu.get_barrier_semaphore()
    for step in range(1, C):
        pl.semaphore_signal(
            barrier, inc=1, device_id=(r, (c + step) % C), device_id_type=MESH
        )

    @pl.when(r > 0)
    def _():
        pl.semaphore_signal(barrier, inc=1, device_id=(r - 1, c), device_id_type=MESH)

    @pl.when(r < R - 1)
    def _():
        pl.semaphore_signal(barrier, inc=1, device_id=(r + 1, c), device_id_type=MESH)

    ends = (R - 1 - r) // (R - 1) + r // (R - 1)
    pl.semaphore_wait(barrier, C + 1 - ends)

    def to_chip(k, s):
        there = q
        bit = 1
        while bit < chips:
            if k & bit:
                there = flip(there, bit)
            bit *= 2
        return pltpu.make_async_remote_copy(
            src_ref=place(q, s, core),
            dst_ref=place(q, s, core),
            send_sem=gather_send,
            recv_sem=gather_recv.at[q, s],
            device_id=(r, 2 * there + core),
            device_id_type=MESH,
        )

    def to_sibling(group, s):
        return pltpu.make_async_remote_copy(
            src_ref=place(group, s, core),
            dst_ref=place(group, s, core),
            send_sem=gather_send,
            recv_sem=sib_recv.at[group, s],
            device_id=(r, sibling),
            device_id_type=MESH,
        )

    near = [1 << i for i in range(chips.bit_length() - 1)]
    far = [k for k in range(1, chips) if k not in near]

    def send_far():
        for s in range(SUBS):
            for k in far:
                to_chip(k, s).start()

    def fetch(slices):
        for group, s in slices:

            @pl.when(group != q)
            def _():
                here = place(group, s, core)
                pltpu.make_async_copy(here, here, gather_recv.at[group, s]).wait()
                to_sibling(group, s).start()

    beside, above = flip(q, 1), flip(q, 2)
    corner = flip(beside, 2)

    def relay(group, s, there):
        pltpu.make_async_remote_copy(
            src_ref=place(group, s, core),
            dst_ref=place(group, s, core),
            send_sem=gather_send,
            recv_sem=gather_recv.at[group, s],
            device_id=(r, 2 * there + core),
            device_id_type=MESH,
        ).start()

    def near_arrives(turn):
        s = TURNS[turn]
        for group in (beside, above):
            here = place(group, s, core)
            pltpu.make_async_copy(here, here, gather_recv.at[group, s]).wait()
            to_sibling(group, s).start()
        if turn % 2 == 0:
            relay(beside, s, above)
        else:
            relay(above, s, beside)

    def corner_arrives(turn):
        s = TURNS[turn]
        here = place(corner, s, core)
        pltpu.make_async_copy(here, here, gather_recv.at[corner, s]).wait()
        to_sibling(corner, s).start()

    def fetched(slices):
        for group, s in slices:
            there = place(group, s, 1 - core)
            pltpu.make_async_copy(there, there, sib_recv.at[group, s]).wait()

    for s in TURNS:
        for k in reversed(near):
            to_chip(k, s).start()
        to_sibling(q, s).start()

    def columns(who):
        return pl.ds(pl.multiple_of(who * width, width), width)

    def slab_of(s):
        return pl.ds(pl.multiple_of(s * slab, slab), slab)

    def add_arrived(slot, s, tile, at):
        block = recv_q.at[slot, tile, slab_of(s)]
        scale = recv_s.at[slot, s, tile]
        pltpu.make_async_copy(block, block, zq_recv.at[slot, s, tile]).wait()
        pltpu.make_async_copy(scale, scale, zs_recv.at[slot, s, tile]).wait()
        lanes = jnp.concatenate([scale[...]] * (width // LANES), axis=1)
        acc[pl.ds(at, slab)] += block[...].astype(jnp.int32).astype(jnp.float32) * lanes

    def pass_on(group, s, tile, at):
        x = acc[pl.ds(at, slab)]
        peak = jnp.max(jnp.abs(x), axis=0, keepdims=True)
        most = peak[:, 0:LANES]
        for j in range(1, width // LANES):
            most = jnp.maximum(most, peak[:, j * LANES : (j + 1) * LANES])
        most = jnp.maximum(most, 1e-30)
        send_s[group, s, tile] = most * (1.0 / STEPS)
        steps = jnp.concatenate([STEPS / most] * (width // LANES), axis=1)
        send_q[group, tile, slab_of(s)] = (
            jnp.round(x * steps).astype(jnp.int32).astype(jnp.int16)
        )

        def copies(target, slot):
            pltpu.make_async_remote_copy(
                src_ref=send_q.at[group, tile, slab_of(s)],
                dst_ref=recv_q.at[slot, tile, slab_of(s)],
                send_sem=zq_send,
                recv_sem=zq_recv.at[slot, s, tile],
                device_id=(target, c),
                device_id_type=MESH,
            ).start()
            pltpu.make_async_remote_copy(
                src_ref=send_s.at[group, s, tile],
                dst_ref=recv_s.at[slot, s, tile],
                send_sem=zs_send,
                recv_sem=zs_recv.at[slot, s, tile],
                device_id=(target, c),
                device_id_type=MESH,
            ).start()

        @pl.when(group > r)
        def _():
            copies(r + 1, group)

        @pl.when(group < r - 1)
        def _():
            copies(r - 1, group)

        @pl.when(group == r - 1)
        def _():
            copies(r - 1, R)

    def deliver(s, tile, at):
        fin[tile, slab_of(s)] = acc[pl.ds(at, slab)].astype(jnp.bfloat16)
        for inside in range(0, slab, share):
            first = pl.multiple_of(s * slab + inside, share)
            source = fin.at[tile, pl.ds(first, share)]
            target = (inside // sub * SUBS + s) * (sub // share) + inside % sub // share

            @pl.when(target != c)
            def _():
                pltpu.make_async_remote_copy(
                    src_ref=source,
                    dst_ref=out_ref.at[tile, :, columns(c)],
                    send_sem=out_send,
                    recv_sem=out_recv,
                    device_id=(r, target),
                    device_id_type=MESH,
                ).start()

            @pl.when(target == c)
            def _():
                pltpu.make_async_copy(
                    source, out_ref.at[tile, :, columns(c)], out_recv
                ).start()

    def unit(slices, hooks):
        @pl.loop(0, tiles)
        def _(tile):
            for i, (group, s) in enumerate(slices):
                work[tile, pl.ds(i * slab, slab)] = held[tile, group, slab_of(s)]

        @pl.loop(0, tiles)
        def _(tile):
            for at, steps in hooks:

                @pl.when(tile == at)
                def _():
                    for step in steps:
                        step()

            total = None
            for j in range(per):
                part = jnp.dot(
                    work[order[1, tile * per + j], pl.ds(0, slab * len(slices))],
                    blocks_vmem[order[0, tile * per + j]],
                    preferred_element_type=jnp.float32,
                )
                total = part if total is None else total + part
            acc[pl.ds(0, slab * len(slices))] = total
            for i, (group, s) in enumerate(slices):
                at = i * slab

                @pl.when(
                    jnp.logical_or(
                        jnp.logical_and(group >= r, r > 0),
                        jnp.logical_and(group < r, r < R - 1),
                    )
                )
                def _():
                    add_arrived(group, s, tile, at)

                @pl.when(jnp.logical_and(group == r, r < R - 1))
                def _():
                    add_arrived(R, s, tile, at)

                @pl.when(group != r)
                def _():
                    pass_on(group, s, tile, at)

                @pl.when(group == r)
                def _():
                    deliver(s, tile, at)

    def run(slices, counts, hooks):
        first = 0
        for number, n in enumerate(counts):
            one = slices[first : first + n]
            first += n
            for at, steps in hooks[number]:
                if at < 0:
                    for step in steps:
                        step()
            fetched(one)
            unit(one, [hook for hook in hooks[number] if hook[0] >= 0])

    def steps(function, *turns):
        return [functools.partial(function, turn) for turn in turns]

    upper = r // (R // 2)
    outer = q * (chips - 1 - q) == 0
    hurried = q + upper * (chips - 1 - 2 * q) == 0

    def corner_if(condition, *turns):
        def step():
            @pl.when(condition)
            def _():
                for turn in turns:
                    corner_arrives(turn)

        return [step]

    if R == 4:
        at_end = r * (R - 1 - r) == 0
        last = tiles - 1

        @pl.when(at_end)
        def _():
            hooks = [[] for _ in END_UNITS]
            hooks[0] = [(-1, steps(near_arrives, 0)), (last, steps(near_arrives, 1))]
            hooks[1] = [(last // 2, steps(near_arrives, 2)), (last, steps(near_arrives, 3))]
            hooks[1][1][1].extend(corner_if(hurried, 0, 1))
            hooks[2] = [
                (
                    last,
                    corner_if(hurried, 2, 3) + corner_if(jnp.logical_not(hurried), 0, 1),
                )
            ]
            hooks[3] = [(last, corner_if(jnp.logical_not(hurried), 2, 3))]
            hooks[0][0][1].append(blocks_copy.wait)
            run(slices_in_order(END_ORDER, r, q), END_UNITS, hooks)

        @pl.when(jnp.logical_not(at_end))
        def _():
            hooks = [[] for _ in INNER_UNITS]
            hooks[0] = [(-1, steps(near_arrives, 0, 1)), (last, steps(near_arrives, 2))]
            hooks[1] = [
                (last // 2, steps(near_arrives, 3)),
                (last, corner_if(outer, 0, 1)),
            ]
            hooks[2] = [
                (last // 2, corner_if(jnp.logical_not(outer), 0, 1)),
                (last, steps(corner_arrives, 2, 3)),
            ]
            hooks[0][0][1].append(blocks_copy.wait)
            run(slices_in_order(INNER_ORDER, r, q), INNER_UNITS, hooks)

    else:
        send_far()
        groups = [[(g + 0 * r, s) for s in range(SUBS)] for g in range(R)]
        hooks = [[(-1, [functools.partial(fetch, group)])] for group in groups]
        hooks[0][0][1].append(blocks_copy.wait)
        run(sum(groups, []), (SUBS,) * R, hooks)

    sent = held.at[:, :, pl.ds(0, rows - rows // C)]
    pltpu.make_async_copy(sent, sent, gather_send).wait()
    sent = send_q.at[pl.ds(0, R - 1)]
    pltpu.make_async_copy(sent, sent, zq_send).wait()
    sent = send_s.at[pl.ds(0, R - 1)]
    pltpu.make_async_copy(sent, sent, zs_send).wait()
    sent = out_ref.at[:, :, pl.ds(0, (C - 1) * width)]
    pltpu.make_async_copy(sent, sent, out_send).wait()
    pltpu.make_async_copy(out_ref, out_ref, out_recv).wait()


def on_device(R, C, amplitudes, integrals, blocks):
    pairs, tiles, inner = amplitudes.shape
    count, _, width = integrals.shape
    per = count // tiles
    share = pairs // R
    sub = pairs // SUBS
    rows = 2 * pairs
    assert C == 2 * R and sub % share == 0 and share % 16 == 0

    key = blocks[:, 1] * count + jnp.arange(count, dtype=jnp.int32)
    rank = jnp.sum((key[:, None] > key[None, :]).astype(jnp.int32), axis=1)
    at = rank[:, None] == jnp.arange(count, dtype=jnp.int32)[None, :]
    both = jnp.stack([jnp.arange(count, dtype=jnp.int32), blocks[:, 0]], axis=0)
    order = jnp.sum(jnp.where(at[None], both[:, :, None], 0), axis=1)

    dma = pltpu.SemaphoreType.DMA
    out = pl.pallas_call(
        functools.partial(kernel, (R, C, tiles, per, sub)),
        out_shape=jax.ShapeDtypeStruct((tiles, share, C * width), jnp.bfloat16),
        in_specs=[
            pl.BlockSpec(memory_space=pltpu.SMEM),
            pl.BlockSpec(memory_space=pl.ANY),
            pl.BlockSpec(memory_space=pl.ANY),
        ],
        out_specs=pl.BlockSpec(memory_space=pltpu.VMEM),
        scratch_shapes=[
            pltpu.VMEM((tiles, R, rows, inner), jnp.bfloat16),
            pltpu.VMEM((tiles, rows, inner), jnp.bfloat16),
            pltpu.VMEM(integrals.shape, jnp.bfloat16),
            pltpu.VMEM((rows, width), jnp.float32),
            pltpu.VMEM((tiles, rows, width), jnp.bfloat16),
            pltpu.VMEM((R, tiles, rows, width), jnp.int16),
            pltpu.VMEM((R + 1, tiles, rows, width), jnp.int16),
            pltpu.VMEM((R, SUBS, tiles, 1, LANES), jnp.float32),
            pltpu.VMEM((R + 1, SUBS, tiles, 1, LANES), jnp.float32),
            dma,
            dma,
            dma((R, SUBS)),
            dma((R, SUBS)),
            dma,
            dma,
            dma((R + 1, SUBS, tiles)),
            dma((R + 1, SUBS, tiles)),
            dma,
            dma,
        ],
        compiler_params=pltpu.CompilerParams(
            collective_id=0, has_side_effects=True, vmem_limit_bytes=67043328
        ),
    )(order, amplitudes.transpose(1, 0, 2), integrals)
    return out.transpose(1, 0, 2)


def solution(mesh):
    return jax.shard_map(
        functools.partial(on_device, mesh.shape["row"], mesh.shape["col"]),
        mesh=mesh,
        in_specs=(P("col", None, "row"), P(None, "row", "col"), P()),
        out_specs=P(("row", "col"), None, None),
        check_vma=False,
    )
```

```python
import functools

import jax
import jax.numpy as jnp
from jax import lax
from jax.experimental import pallas as pl
from jax.experimental.pallas import tpu as pltpu
from jax.sharding import PartitionSpec as P

MESH = pl.DeviceIdType.MESH
STEPS = 32767.0
LANES = 128
SUBS = 4
TURNS = (0, 2, 1, 3)
END_UNITS = (2, 2, 2, 2, 2, 2, 2, 2)
END_ORDER = (
    (8, 4, 9, 5, 12, 13, 14, 15, 10, 11, 0, 1, 6, 7, 2, 3),
    (4, 5, 12, 13, 14, 15, 8, 9, 10, 11, 0, 1, 6, 7, 2, 3),
    (8, 9, 12, 13, 14, 15, 10, 11, 4, 5, 0, 1, 6, 7, 2, 3),
    (12, 13, 14, 15, 8, 9, 10, 11, 4, 5, 0, 1, 6, 7, 2, 3),
)
INNER_UNITS = (2, 2, 4, 4, 2, 2)
INNER_ORDER = (
    (8, 0, 9, 1, 12, 13, 2, 3, 14, 15, 4, 5, 10, 11, 6, 7),
    (12, 13, 4, 5, 14, 15, 0, 1, 8, 9, 2, 3, 10, 11, 6, 7),
    (8, 9, 12, 13, 14, 15, 0, 1, 10, 11, 2, 3, 4, 5, 6, 7),
    (12, 13, 14, 15, 8, 9, 0, 1, 10, 11, 2, 3, 4, 5, 6, 7),
)


def flip(index, bit):
    return index + bit - 2 * bit * ((index // bit) % 2)


def slices_in_order(table, r, q):
    upper = r // 2
    chip = q + upper * (3 - 2 * q)
    low, high = chip % 2, chip // 2
    slices = []
    for codes in zip(*table):
        a, b, c, d = (SUBS * (x // SUBS) + TURNS[x % SUBS] for x in codes)
        code = a + low * (b - a) + high * (c - a) + low * high * (a + d - b - c)
        group, s = code // SUBS, code % SUBS
        slices.append((group + upper * (3 - 2 * group), s))
    return slices


def sort_blocks(tiles, per, table_ref, order, filled):
    for tile in range(tiles):
        filled[tile] = 0

    @pl.loop(0, tiles * per)
    def _(block):
        tile = table_ref[1, block]
        at = filled[tile]
        order[0, tile * per + at] = block
        order[1, tile * per + at] = table_ref[0, block]
        filled[tile] = at + 1


def kernel(
    sizes,
    order,
    amp_ref,
    int_ref,
    out_ref,
    held,
    native,
    work,
    blocks_vmem,
    acc,
    fin,
    send_q,
    recv_q,
    send_s,
    recv_s,
    amp_sem,
    int_sem,
    gather_send,
    gather_recv,
    sib_recv,
    zq_send,
    zs_send,
    zq_recv,
    zs_recv,
    out_send,
    out_recv,
):
    R, C, tiles, per, sub = sizes
    chips = C // 2
    rows, inner = held.shape[2:]
    slab = 2 * sub
    width = acc.shape[1]
    share = out_ref.shape[1]

    r = lax.axis_index("row")
    c = lax.axis_index("col")
    q = c // 2
    core = c % 2
    sibling = 2 * q + 1 - core

    def place(group, s, of_core):
        first = pl.multiple_of((2 * s + of_core) * sub, sub)
        return held.at[:, group, pl.ds(first, sub)]

    amp_copy = pltpu.make_async_copy(amp_ref, native, amp_sem)
    amp_copy.start()
    amp_copy.wait()
    blocks_copy = pltpu.make_async_copy(int_ref, blocks_vmem, int_sem)
    blocks_copy.start()

    barrier = pltpu.get_barrier_semaphore()
    for step in range(1, C):
        pl.semaphore_signal(
            barrier, inc=1, device_id=(r, (c + step) % C), device_id_type=MESH
        )

    @pl.when(r > 0)
    def _():
        pl.semaphore_signal(barrier, inc=1, device_id=(r - 1, c), device_id_type=MESH)

    @pl.when(r < R - 1)
    def _():
        pl.semaphore_signal(barrier, inc=1, device_id=(r + 1, c), device_id_type=MESH)

    ends = (R - 1 - r) // (R - 1) + r // (R - 1)
    pl.semaphore_wait(barrier, C + 1 - ends)

    def to_chip(k, s):
        there = q
        bit = 1
        while bit < chips:
            if k & bit:
                there = flip(there, bit)
            bit *= 2
        return pltpu.make_async_remote_copy(
            src_ref=place(q, s, core),
            dst_ref=place(q, s, core),
            send_sem=gather_send,
            recv_sem=gather_recv.at[q, s],
            device_id=(r, 2 * there + core),
            device_id_type=MESH,
        )

    def to_sibling(group, s):
        return pltpu.make_async_remote_copy(
            src_ref=place(group, s, core),
            dst_ref=place(group, s, core),
            send_sem=gather_send,
            recv_sem=sib_recv.at[group, s],
            device_id=(r, sibling),
            device_id_type=MESH,
        )

    near = [1 << i for i in range(chips.bit_length() - 1)]
    far = [k for k in range(1, chips) if k not in near]

    def send_far():
        for s in range(SUBS):
            for k in far:
                to_chip(k, s).start()

    def fetch(slices):
        for group, s in slices:

            @pl.when(group != q)
            def _():
                here = place(group, s, core)
                pltpu.make_async_copy(here, here, gather_recv.at[group, s]).wait()
                to_sibling(group, s).start()

    beside, above = flip(q, 1), flip(q, 2)
    corner = flip(beside, 2)

    def relay(group, s, there):
        pltpu.make_async_remote_copy(
            src_ref=place(group, s, core),
            dst_ref=place(group, s, core),
            send_sem=gather_send,
            recv_sem=gather_recv.at[group, s],
            device_id=(r, 2 * there + core),
            device_id_type=MESH,
        ).start()

    def near_arrives(turn):
        s = TURNS[turn]
        for group in (beside, above):
            here = place(group, s, core)
            pltpu.make_async_copy(here, here, gather_recv.at[group, s]).wait()
            to_sibling(group, s).start()
        if turn % 2 == 0:
            relay(beside, s, above)
        else:
            relay(above, s, beside)

    def corner_arrives(turn):
        s = TURNS[turn]
        here = place(corner, s, core)
        pltpu.make_async_copy(here, here, gather_recv.at[corner, s]).wait()
        to_sibling(corner, s).start()

    def fetched(slices):
        for group, s in slices:
            there = place(group, s, 1 - core)
            pltpu.make_async_copy(there, there, sib_recv.at[group, s]).wait()

    for s in TURNS:
        first = pl.multiple_of((2 * s + core) * sub, sub)
        for at in range(0, inner, LANES):
            part = native[pl.ds(s * sub, sub), :, pl.ds(at, LANES)].astype(jnp.float32)
            part = part.transpose(1, 0, 2).astype(jnp.bfloat16)
            held[:, q, pl.ds(first, sub), pl.ds(at, LANES)] = part
        for k in reversed(near):
            to_chip(k, s).start()
        to_sibling(q, s).start()

    def columns(who):
        return pl.ds(pl.multiple_of(who * width, width), width)

    def slab_of(s):
        return pl.ds(pl.multiple_of(s * slab, slab), slab)

    def add_arrived(slot, s, tile, at):
        block = recv_q.at[slot, tile, slab_of(s)]
        scale = recv_s.at[slot, s, tile]
        pltpu.make_async_copy(block, block, zq_recv.at[slot, s, tile]).wait()
        pltpu.make_async_copy(scale, scale, zs_recv.at[slot, s, tile]).wait()
        lanes = jnp.concatenate([scale[...]] * (width // LANES), axis=1)
        acc[pl.ds(at, slab)] += block[...].astype(jnp.int32).astype(jnp.float32) * lanes

    def pass_on(group, s, tile, at):
        x = acc[pl.ds(at, slab)]
        peak = jnp.max(jnp.abs(x), axis=0, keepdims=True)
        most = peak[:, 0:LANES]
        for j in range(1, width // LANES):
            most = jnp.maximum(most, peak[:, j * LANES : (j + 1) * LANES])
        most = jnp.maximum(most, 1e-30)
        send_s[group, s, tile] = most * (1.0 / STEPS)
        steps = jnp.concatenate([STEPS / most] * (width // LANES), axis=1)
        send_q[group, tile, slab_of(s)] = (
            jnp.round(x * steps).astype(jnp.int32).astype(jnp.int16)
        )

        def copies(target, slot):
            pltpu.make_async_remote_copy(
                src_ref=send_q.at[group, tile, slab_of(s)],
                dst_ref=recv_q.at[slot, tile, slab_of(s)],
                send_sem=zq_send,
                recv_sem=zq_recv.at[slot, s, tile],
                device_id=(target, c),
                device_id_type=MESH,
            ).start()
            pltpu.make_async_remote_copy(
                src_ref=send_s.at[group, s, tile],
                dst_ref=recv_s.at[slot, s, tile],
                send_sem=zs_send,
                recv_sem=zs_recv.at[slot, s, tile],
                device_id=(target, c),
                device_id_type=MESH,
            ).start()

        @pl.when(group > r)
        def _():
            copies(r + 1, group)

        @pl.when(group < r - 1)
        def _():
            copies(r - 1, group)

        @pl.when(group == r - 1)
        def _():
            copies(r - 1, R)

    def deliver(s, tile, at):
        fin[tile, slab_of(s)] = acc[pl.ds(at, slab)].astype(jnp.bfloat16)
        for inside in range(0, slab, share):
            first = pl.multiple_of(s * slab + inside, share)
            source = fin.at[tile, pl.ds(first, share)]
            target = (inside // sub * SUBS + s) * (sub // share) + inside % sub // share

            @pl.when(target != c)
            def _():
                pltpu.make_async_remote_copy(
                    src_ref=source,
                    dst_ref=out_ref.at[tile, :, columns(c)],
                    send_sem=out_send,
                    recv_sem=out_recv,
                    device_id=(r, target),
                    device_id_type=MESH,
                ).start()

            @pl.when(target == c)
            def _():
                pltpu.make_async_copy(
                    source, out_ref.at[tile, :, columns(c)], out_recv
                ).start()

    def unit(slices, hooks):
        @pl.loop(0, tiles)
        def _(tile):
            for i, (group, s) in enumerate(slices):
                work[tile, pl.ds(i * slab, slab)] = held[tile, group, slab_of(s)]

        @pl.loop(0, tiles)
        def _(tile):
            for at, steps in hooks:

                @pl.when(tile == at)
                def _():
                    for step in steps:
                        step()

            total = None
            for j in range(per):
                part = jnp.dot(
                    work[order[1, tile * per + j], pl.ds(0, slab * len(slices))],
                    blocks_vmem[order[0, tile * per + j]],
                    preferred_element_type=jnp.float32,
                )
                total = part if total is None else total + part
            acc[pl.ds(0, slab * len(slices))] = total
            for i, (group, s) in enumerate(slices):
                at = i * slab

                @pl.when(
                    jnp.logical_or(
                        jnp.logical_and(group >= r, r > 0),
                        jnp.logical_and(group < r, r < R - 1),
                    )
                )
                def _():
                    add_arrived(group, s, tile, at)

                @pl.when(jnp.logical_and(group == r, r < R - 1))
                def _():
                    add_arrived(R, s, tile, at)

                @pl.when(group != r)
                def _():
                    pass_on(group, s, tile, at)

                @pl.when(group == r)
                def _():
                    deliver(s, tile, at)

    def run(slices, counts, hooks):
        first = 0
        for number, n in enumerate(counts):
            one = slices[first : first + n]
            first += n
            for at, steps in hooks[number]:
                if at < 0:
                    for step in steps:
                        step()
            fetched(one)
            unit(one, [hook for hook in hooks[number] if hook[0] >= 0])

    def steps(function, *turns):
        return [functools.partial(function, turn) for turn in turns]

    upper = r // (R // 2)
    outer = q * (chips - 1 - q) == 0
    hurried = q + upper * (chips - 1 - 2 * q) == 0

    def corner_if(condition, *turns):
        def step():
            @pl.when(condition)
            def _():
                for turn in turns:
                    corner_arrives(turn)

        return [step]

    if R == 4:
        at_end = r * (R - 1 - r) == 0
        last = tiles - 1

        @pl.when(at_end)
        def _():
            hooks = [[] for _ in END_UNITS]
            hooks[0] = [(-1, steps(near_arrives, 0)), (last, steps(near_arrives, 1))]
            hooks[1] = [(last // 2, steps(near_arrives, 2)), (last, steps(near_arrives, 3))]
            hooks[1][1][1].extend(corner_if(hurried, 0, 1))
            hooks[2] = [
                (
                    last,
                    corner_if(hurried, 2, 3) + corner_if(jnp.logical_not(hurried), 0, 1),
                )
            ]
            hooks[3] = [(last, corner_if(jnp.logical_not(hurried), 2, 3))]
            hooks[0][0][1].append(blocks_copy.wait)
            run(slices_in_order(END_ORDER, r, q), END_UNITS, hooks)

        @pl.when(jnp.logical_not(at_end))
        def _():
            hooks = [[] for _ in INNER_UNITS]
            hooks[0] = [(-1, steps(near_arrives, 0, 1)), (last, steps(near_arrives, 2))]
            hooks[1] = [
                (last // 2, steps(near_arrives, 3)),
                (last, corner_if(outer, 0, 1)),
            ]
            hooks[2] = [
                (last // 2, corner_if(jnp.logical_not(outer), 0, 1)),
                (last, steps(corner_arrives, 2, 3)),
            ]
            hooks[0][0][1].append(blocks_copy.wait)
            run(slices_in_order(INNER_ORDER, r, q), INNER_UNITS, hooks)

    else:
        send_far()
        groups = [[(g + 0 * r, s) for s in range(SUBS)] for g in range(R)]
        hooks = [[(-1, [functools.partial(fetch, group)])] for group in groups]
        hooks[0][0][1].append(blocks_copy.wait)
        run(sum(groups, []), (SUBS,) * R, hooks)

    sent = held.at[:, :, pl.ds(0, rows - rows // C)]
    pltpu.make_async_copy(sent, sent, gather_send).wait()
    sent = send_q.at[pl.ds(0, R - 1)]
    pltpu.make_async_copy(sent, sent, zq_send).wait()
    sent = send_s.at[pl.ds(0, R - 1)]
    pltpu.make_async_copy(sent, sent, zs_send).wait()
    sent = out_ref.at[:, :, pl.ds(0, (C - 1) * width)]
    pltpu.make_async_copy(sent, sent, out_send).wait()
    pltpu.make_async_copy(out_ref, out_ref, out_recv).wait()


def on_device(R, C, amplitudes, integrals, blocks):
    pairs, tiles, inner = amplitudes.shape
    count, _, width = integrals.shape
    per = count // tiles
    share = pairs // R
    sub = pairs // SUBS
    rows = 2 * pairs
    assert C == 2 * R and sub % share == 0 and share % 16 == 0

    order = pl.pallas_call(
        functools.partial(sort_blocks, tiles, per),
        out_shape=jax.ShapeDtypeStruct((2, count), jnp.int32),
        in_specs=[pl.BlockSpec(memory_space=pltpu.SMEM)],
        out_specs=pl.BlockSpec(memory_space=pltpu.SMEM),
        scratch_shapes=[pltpu.SMEM((tiles,), jnp.int32)],
    )(blocks.T)

    dma = pltpu.SemaphoreType.DMA
    out = pl.pallas_call(
        functools.partial(kernel, (R, C, tiles, per, sub)),
        out_shape=jax.ShapeDtypeStruct((tiles, share, C * width), jnp.bfloat16),
        in_specs=[
            pl.BlockSpec(memory_space=pltpu.SMEM),
            pl.BlockSpec(memory_space=pl.ANY),
            pl.BlockSpec(memory_space=pl.ANY),
        ],
        out_specs=pl.BlockSpec(memory_space=pltpu.VMEM),
        scratch_shapes=[
            pltpu.VMEM((tiles, R, rows, inner), jnp.bfloat16),
            pltpu.VMEM(amplitudes.shape, jnp.bfloat16),
            pltpu.VMEM((tiles, rows, inner), jnp.bfloat16),
            pltpu.VMEM(integrals.shape, jnp.bfloat16),
            pltpu.VMEM((rows, width), jnp.float32),
            pltpu.VMEM((tiles, rows, width), jnp.bfloat16),
            pltpu.VMEM((R, tiles, rows, width), jnp.int16),
            pltpu.VMEM((R + 1, tiles, rows, width), jnp.int16),
            pltpu.VMEM((R, SUBS, tiles, 1, LANES), jnp.float32),
            pltpu.VMEM((R + 1, SUBS, tiles, 1, LANES), jnp.float32),
            dma,
            dma,
            dma,
            dma((R, SUBS)),
            dma((R, SUBS)),
            dma,
            dma,
            dma((R + 1, SUBS, tiles)),
            dma((R + 1, SUBS, tiles)),
            dma,
            dma,
        ],
        compiler_params=pltpu.CompilerParams(
            collective_id=0, has_side_effects=True, vmem_limit_bytes=67043328
        ),
    )(order, amplitudes, integrals)
    return out.transpose(1, 0, 2)


def solution(mesh):
    return jax.shard_map(
        functools.partial(on_device, mesh.shape["row"], mesh.shape["col"]),
        mesh=mesh,
        in_specs=(P("col", None, "row"), P(None, "row", "col"), P()),
        out_specs=P(("row", "col"), None, None),
        check_vma=False,
    )
```

```python
import functools

import jax
import jax.numpy as jnp
from jax import lax
from jax.experimental import pallas as pl
from jax.experimental.pallas import tpu as pltpu
from jax.sharding import PartitionSpec as P

MESH = pl.DeviceIdType.MESH
STEPS = 32767.0
LANES = 128
SUBS = 4
TURNS = (0, 2, 1, 3)
END_UNITS = (2, 2, 2, 2, 2, 2, 2, 2)
END_ORDER = (
    (8, 4, 9, 5, 12, 13, 14, 15, 10, 11, 0, 1, 6, 7, 2, 3),
    (4, 5, 12, 13, 14, 15, 8, 9, 10, 11, 0, 1, 6, 7, 2, 3),
    (8, 9, 12, 13, 14, 15, 10, 11, 4, 5, 0, 1, 6, 7, 2, 3),
    (12, 13, 14, 15, 8, 9, 10, 11, 4, 5, 0, 1, 6, 7, 2, 3),
)
INNER_UNITS = (2, 2, 4, 4, 2, 2)
INNER_ORDER = (
    (8, 0, 9, 1, 12, 13, 2, 3, 14, 15, 4, 5, 10, 11, 6, 7),
    (12, 13, 4, 5, 14, 15, 0, 1, 8, 9, 2, 3, 10, 11, 6, 7),
    (8, 9, 12, 13, 14, 15, 0, 1, 10, 11, 2, 3, 4, 5, 6, 7),
    (12, 13, 14, 15, 8, 9, 0, 1, 10, 11, 2, 3, 4, 5, 6, 7),
)


def flip(index, bit):
    return index + bit - 2 * bit * ((index // bit) % 2)


def slices_in_order(table, r, q):
    upper = r // 2
    chip = q + upper * (3 - 2 * q)
    low, high = chip % 2, chip // 2
    slices = []
    for codes in zip(*table):
        a, b, c, d = (SUBS * (x // SUBS) + TURNS[x % SUBS] for x in codes)
        code = a + low * (b - a) + high * (c - a) + low * high * (a + d - b - c)
        group, s = code // SUBS, code % SUBS
        slices.append((group + upper * (3 - 2 * group), s))
    return slices


def sort_blocks(tiles, per, table_ref, order, filled):
    for tile in range(tiles):
        filled[tile] = 0

    @pl.loop(0, tiles * per)
    def _(block):
        tile = table_ref[1, block]
        at = filled[tile]
        order[0, tile * per + at] = block
        order[1, tile * per + at] = table_ref[0, block]
        filled[tile] = at + 1


def kernel(
    sizes,
    order,
    amp_ref,
    int_ref,
    out_ref,
    held,
    native,
    work,
    blocks_vmem,
    acc,
    fin,
    send_q,
    recv_q,
    send_s,
    recv_s,
    amp_sem,
    int_sem,
    gather_send,
    gather_recv,
    sib_recv,
    zq_send,
    zs_send,
    zq_recv,
    zs_recv,
    out_send,
    out_recv,
):
    R, C, tiles, per, sub = sizes
    chips = C // 2
    rows, inner = held.shape[2:]
    slab = 2 * sub
    width = acc.shape[1]
    share = out_ref.shape[1]

    r = lax.axis_index("row")
    c = lax.axis_index("col")
    q = c // 2
    core = c % 2
    sibling = 2 * q + 1 - core

    def place(group, s, of_core):
        first = pl.multiple_of((2 * s + of_core) * sub, sub)
        return held.at[:, group, pl.ds(first, sub)]

    amp_copy = pltpu.make_async_copy(amp_ref, native, amp_sem)
    amp_copy.start()
    barrier = pltpu.get_barrier_semaphore()
    for step in range(1, C):
        pl.semaphore_signal(
            barrier, inc=1, device_id=(r, (c + step) % C), device_id_type=MESH
        )

    @pl.when(r > 0)
    def _():
        pl.semaphore_signal(barrier, inc=1, device_id=(r - 1, c), device_id_type=MESH)

    @pl.when(r < R - 1)
    def _():
        pl.semaphore_signal(barrier, inc=1, device_id=(r + 1, c), device_id_type=MESH)

    amp_copy.wait()
    blocks_copy = pltpu.make_async_copy(int_ref, blocks_vmem, int_sem)
    blocks_copy.start()

    def to_chip(k, s):
        there = q
        bit = 1
        while bit < chips:
            if k & bit:
                there = flip(there, bit)
            bit *= 2
        return pltpu.make_async_remote_copy(
            src_ref=place(q, s, core),
            dst_ref=place(q, s, core),
            send_sem=gather_send,
            recv_sem=gather_recv.at[q, s],
            device_id=(r, 2 * there + core),
            device_id_type=MESH,
        )

    def to_sibling(group, s):
        return pltpu.make_async_remote_copy(
            src_ref=place(group, s, core),
            dst_ref=place(group, s, core),
            send_sem=gather_send,
            recv_sem=sib_recv.at[group, s],
            device_id=(r, sibling),
            device_id_type=MESH,
        )

    near = [1 << i for i in range(chips.bit_length() - 1)]
    far = [k for k in range(1, chips) if k not in near]

    def send_far():
        for s in range(SUBS):
            for k in far:
                to_chip(k, s).start()

    def fetch(slices):
        for group, s in slices:

            @pl.when(group != q)
            def _():
                here = place(group, s, core)
                pltpu.make_async_copy(here, here, gather_recv.at[group, s]).wait()
                to_sibling(group, s).start()

    beside, above = flip(q, 1), flip(q, 2)
    corner = flip(beside, 2)

    def relay(group, s, there):
        pltpu.make_async_remote_copy(
            src_ref=place(group, s, core),
            dst_ref=place(group, s, core),
            send_sem=gather_send,
            recv_sem=gather_recv.at[group, s],
            device_id=(r, 2 * there + core),
            device_id_type=MESH,
        ).start()

    def near_arrives(turn):
        s = TURNS[turn]
        for group in (beside, above):
            here = place(group, s, core)
            pltpu.make_async_copy(here, here, gather_recv.at[group, s]).wait()
            to_sibling(group, s).start()
        if turn % 2 == 0:
            relay(beside, s, above)
        else:
            relay(above, s, beside)

    def corner_arrives(turn):
        s = TURNS[turn]
        here = place(corner, s, core)
        pltpu.make_async_copy(here, here, gather_recv.at[corner, s]).wait()
        to_sibling(corner, s).start()

    def fetched(slices):
        for group, s in slices:
            there = place(group, s, 1 - core)
            pltpu.make_async_copy(there, there, sib_recv.at[group, s]).wait()

    for s in TURNS:
        first = pl.multiple_of((2 * s + core) * sub, sub)
        for at in range(0, inner, LANES):
            part = native[pl.ds(s * sub, sub), :, pl.ds(at, LANES)].astype(jnp.float32)
            part = part.transpose(1, 0, 2).astype(jnp.bfloat16)
            held[:, q, pl.ds(first, sub), pl.ds(at, LANES)] = part
        if s == TURNS[0]:
            ends = (R - 1 - r) // (R - 1) + r // (R - 1)
            pl.semaphore_wait(barrier, C + 1 - ends)
        for k in reversed(near):
            to_chip(k, s).start()
        to_sibling(q, s).start()

    def columns(who):
        return pl.ds(pl.multiple_of(who * width, width), width)

    def slab_of(s):
        return pl.ds(pl.multiple_of(s * slab, slab), slab)

    def add_arrived(slot, s, tile, at):
        block = recv_q.at[slot, tile, slab_of(s)]
        scale = recv_s.at[slot, s, tile]
        pltpu.make_async_copy(block, block, zq_recv.at[slot, s, tile]).wait()
        pltpu.make_async_copy(scale, scale, zs_recv.at[slot, s, tile]).wait()
        lanes = jnp.concatenate([scale[...]] * (width // LANES), axis=1)
        acc[pl.ds(at, slab)] += block[...].astype(jnp.int32).astype(jnp.float32) * lanes

    def pass_on(group, s, tile, at):
        x = acc[pl.ds(at, slab)]
        peak = jnp.max(jnp.abs(x), axis=0, keepdims=True)
        most = peak[:, 0:LANES]
        for j in range(1, width // LANES):
            most = jnp.maximum(most, peak[:, j * LANES : (j + 1) * LANES])
        most = jnp.maximum(most, 1e-30)
        send_s[group, s, tile] = most * (1.0 / STEPS)
        steps = jnp.concatenate([STEPS / most] * (width // LANES), axis=1)
        send_q[group, tile, slab_of(s)] = (
            jnp.round(x * steps).astype(jnp.int32).astype(jnp.int16)
        )

        def copies(target, slot):
            pltpu.make_async_remote_copy(
                src_ref=send_q.at[group, tile, slab_of(s)],
                dst_ref=recv_q.at[slot, tile, slab_of(s)],
                send_sem=zq_send,
                recv_sem=zq_recv.at[slot, s, tile],
                device_id=(target, c),
                device_id_type=MESH,
            ).start()
            pltpu.make_async_remote_copy(
                src_ref=send_s.at[group, s, tile],
                dst_ref=recv_s.at[slot, s, tile],
                send_sem=zs_send,
                recv_sem=zs_recv.at[slot, s, tile],
                device_id=(target, c),
                device_id_type=MESH,
            ).start()

        @pl.when(group > r)
        def _():
            copies(r + 1, group)

        @pl.when(group < r - 1)
        def _():
            copies(r - 1, group)

        @pl.when(group == r - 1)
        def _():
            copies(r - 1, R)

    def deliver(s, tile, at):
        fin[tile, slab_of(s)] = acc[pl.ds(at, slab)].astype(jnp.bfloat16)
        for inside in range(0, slab, share):
            first = pl.multiple_of(s * slab + inside, share)
            source = fin.at[tile, pl.ds(first, share)]
            target = (inside // sub * SUBS + s) * (sub // share) + inside % sub // share

            @pl.when(target != c)
            def _():
                pltpu.make_async_remote_copy(
                    src_ref=source,
                    dst_ref=out_ref.at[tile, :, columns(c)],
                    send_sem=out_send,
                    recv_sem=out_recv,
                    device_id=(r, target),
                    device_id_type=MESH,
                ).start()

            @pl.when(target == c)
            def _():
                pltpu.make_async_copy(
                    source, out_ref.at[tile, :, columns(c)], out_recv
                ).start()

    def unit(slices, hooks):
        @pl.loop(0, tiles)
        def _(tile):
            for i, (group, s) in enumerate(slices):
                work[tile, pl.ds(i * slab, slab)] = held[tile, group, slab_of(s)]

        @pl.loop(0, tiles)
        def _(tile):
            for at, steps in hooks:

                @pl.when(tile == at)
                def _():
                    for step in steps:
                        step()

            total = None
            for j in range(per):
                part = jnp.dot(
                    work[order[1, tile * per + j], pl.ds(0, slab * len(slices))],
                    blocks_vmem[order[0, tile * per + j]],
                    preferred_element_type=jnp.float32,
                )
                total = part if total is None else total + part
            acc[pl.ds(0, slab * len(slices))] = total
            for i, (group, s) in enumerate(slices):
                at = i * slab

                @pl.when(
                    jnp.logical_or(
                        jnp.logical_and(group >= r, r > 0),
                        jnp.logical_and(group < r, r < R - 1),
                    )
                )
                def _():
                    add_arrived(group, s, tile, at)

                @pl.when(jnp.logical_and(group == r, r < R - 1))
                def _():
                    add_arrived(R, s, tile, at)

                @pl.when(group != r)
                def _():
                    pass_on(group, s, tile, at)

                @pl.when(group == r)
                def _():
                    deliver(s, tile, at)

    def run(slices, counts, hooks):
        first = 0
        for number, n in enumerate(counts):
            one = slices[first : first + n]
            first += n
            for at, steps in hooks[number]:
                if at < 0:
                    for step in steps:
                        step()
            fetched(one)
            unit(one, [hook for hook in hooks[number] if hook[0] >= 0])

    def steps(function, *turns):
        return [functools.partial(function, turn) for turn in turns]

    upper = r // (R // 2)
    outer = q * (chips - 1 - q) == 0
    hurried = q + upper * (chips - 1 - 2 * q) == 0

    def corner_if(condition, *turns):
        def step():
            @pl.when(condition)
            def _():
                for turn in turns:
                    corner_arrives(turn)

        return [step]

    if R == 4:
        at_end = r * (R - 1 - r) == 0
        last = tiles - 1

        @pl.when(at_end)
        def _():
            hooks = [[] for _ in END_UNITS]
            hooks[0] = [(-1, steps(near_arrives, 0)), (last, steps(near_arrives, 1))]
            hooks[1] = [(last // 2, steps(near_arrives, 2)), (last, steps(near_arrives, 3))]
            hooks[1][1][1].extend(corner_if(hurried, 0, 1))
            hooks[2] = [
                (
                    last,
                    corner_if(hurried, 2, 3) + corner_if(jnp.logical_not(hurried), 0, 1),
                )
            ]
            hooks[3] = [(last, corner_if(jnp.logical_not(hurried), 2, 3))]
            hooks[0][0][1].append(blocks_copy.wait)
            run(slices_in_order(END_ORDER, r, q), END_UNITS, hooks)

        @pl.when(jnp.logical_not(at_end))
        def _():
            hooks = [[] for _ in INNER_UNITS]
            hooks[0] = [(-1, steps(near_arrives, 0, 1)), (last, steps(near_arrives, 2))]
            hooks[1] = [
                (last // 2, steps(near_arrives, 3)),
                (last, corner_if(outer, 0, 1)),
            ]
            hooks[2] = [
                (last // 2, corner_if(jnp.logical_not(outer), 0, 1)),
                (last, steps(corner_arrives, 2, 3)),
            ]
            hooks[0][0][1].append(blocks_copy.wait)
            run(slices_in_order(INNER_ORDER, r, q), INNER_UNITS, hooks)

    else:
        send_far()
        groups = [[(g + 0 * r, s) for s in range(SUBS)] for g in range(R)]
        hooks = [[(-1, [functools.partial(fetch, group)])] for group in groups]
        hooks[0][0][1].append(blocks_copy.wait)
        run(sum(groups, []), (SUBS,) * R, hooks)

    sent = held.at[:, :, pl.ds(0, rows - rows // C)]
    pltpu.make_async_copy(sent, sent, gather_send).wait()
    sent = send_q.at[pl.ds(0, R - 1)]
    pltpu.make_async_copy(sent, sent, zq_send).wait()
    sent = send_s.at[pl.ds(0, R - 1)]
    pltpu.make_async_copy(sent, sent, zs_send).wait()
    sent = out_ref.at[:, :, pl.ds(0, (C - 1) * width)]
    pltpu.make_async_copy(sent, sent, out_send).wait()
    pltpu.make_async_copy(out_ref, out_ref, out_recv).wait()


def on_device(R, C, amplitudes, integrals, blocks):
    pairs, tiles, inner = amplitudes.shape
    count, _, width = integrals.shape
    per = count // tiles
    share = pairs // R
    sub = pairs // SUBS
    rows = 2 * pairs
    assert C == 2 * R and sub % share == 0 and share % 16 == 0

    order = pl.pallas_call(
        functools.partial(sort_blocks, tiles, per),
        out_shape=jax.ShapeDtypeStruct((2, count), jnp.int32),
        in_specs=[pl.BlockSpec(memory_space=pltpu.SMEM)],
        out_specs=pl.BlockSpec(memory_space=pltpu.SMEM),
        scratch_shapes=[pltpu.SMEM((tiles,), jnp.int32)],
    )(blocks.T)

    dma = pltpu.SemaphoreType.DMA
    out = pl.pallas_call(
        functools.partial(kernel, (R, C, tiles, per, sub)),
        out_shape=jax.ShapeDtypeStruct((tiles, share, C * width), jnp.bfloat16),
        in_specs=[
            pl.BlockSpec(memory_space=pltpu.SMEM),
            pl.BlockSpec(memory_space=pl.ANY),
            pl.BlockSpec(memory_space=pl.ANY),
        ],
        out_specs=pl.BlockSpec(memory_space=pltpu.VMEM),
        scratch_shapes=[
            pltpu.VMEM((tiles, R, rows, inner), jnp.bfloat16),
            pltpu.VMEM(amplitudes.shape, jnp.bfloat16),
            pltpu.VMEM((tiles, rows, inner), jnp.bfloat16),
            pltpu.VMEM(integrals.shape, jnp.bfloat16),
            pltpu.VMEM((rows, width), jnp.float32),
            pltpu.VMEM((tiles, rows, width), jnp.bfloat16),
            pltpu.VMEM((R, tiles, rows, width), jnp.int16),
            pltpu.VMEM((R + 1, tiles, rows, width), jnp.int16),
            pltpu.VMEM((R, SUBS, tiles, 1, LANES), jnp.float32),
            pltpu.VMEM((R + 1, SUBS, tiles, 1, LANES), jnp.float32),
            dma,
            dma,
            dma,
            dma((R, SUBS)),
            dma((R, SUBS)),
            dma,
            dma,
            dma((R + 1, SUBS, tiles)),
            dma((R + 1, SUBS, tiles)),
            dma,
            dma,
        ],
        compiler_params=pltpu.CompilerParams(
            collective_id=0, has_side_effects=True, vmem_limit_bytes=67043328
        ),
    )(order, amplitudes, integrals)
    return out.transpose(1, 0, 2)


def solution(mesh):
    return jax.shard_map(
        functools.partial(on_device, mesh.shape["row"], mesh.shape["col"]),
        mesh=mesh,
        in_specs=(P("col", None, "row"), P(None, "row", "col"), P()),
        out_specs=P(("row", "col"), None, None),
        check_vma=False,
    )
```
